1024 devices in a mesh: bulk: 128 (over x, y, z_hi), owner: 8 (over z_lo, core).
Axes of the slice: x: 8, y: 8, z: 8 (z_hi: 2, z_lo: 4; z = z_hi * 4 + z_lo), core: 2. Of those that a mesh axis runs over, the one named last changes fastest.
Arguments:
- slab_cols: float32 [4096, 8192], P('bulk', 'owner'), may hold values from -6 to 6
- pivots: int32 [8192], replicated, may hold values from 0 to 8191, each once
- lower_panels: bfloat16 [8192, 2048], P('bulk', 'owner'), may hold values from -0.125 to 0.125
- upper_rows: bfloat16 [4096, 2048], P('bulk', 'owner'), may hold values from -6 to 6
Outputs:
- updated: float32 [4096, 8192], P('bulk', 'owner')
The draws below stay inside these ranges and needn't reach their ends.
All inputs are finite; a program needn't handle non-finite values.
Results may differ from the reference program's by a relative error of at most 0.0003.
Values may be sent and summed in bfloat16 or wider, within the bound.
No kernel may reach another device: no remote copies, remote signals or barrier semaphores. Data moves between devices by JAX's collectives and lax.ppermute only.
A program may use at most 32 MiB of HBM per device.

```python
import jax
import jax.numpy as jnp
from jax import lax

SLAB = 4096
INNER = 2048
ROWS = 8192


def block_levels(rng, extent, shards, low, high):
    factor_of, own = 1.0, jax.random.fold_in(rng, 6)
    for position, shards_of in shards:
        steps = jnp.exp(jax.random.uniform(jax.random.fold_in(own, position), (shards_of,), jnp.float32, low / len(shards), high / len(shards)))
        factor_of = factor_of * jnp.repeat(steps, extent[position] // shards_of).reshape([-1 if axis == position else 1 for axis in range(len(extent))])
    return factor_of


def centred(key, extent, scale, bound, pieces=(), held_as=jnp.bfloat16):
    drawn = jax.random.normal(key, extent, jnp.float32) * scale
    if len(pieces) > 0:
        drawn = block_levels(key, extent, pieces, -0.22, 0.18) * drawn
    return jnp.clip(drawn, min=-bound, max=bound).astype(held_as)


def setup_inputs(seed: int = 0) -> dict:
    splits = jax.random.split(jax.random.key(seed), 5)
    slab_cols = centred(splits[0], (SLAB, ROWS), 1.0, 6.0, ((0, 128), (1, 8)), jnp.float32)
    pivots = jax.random.permutation(splits[1], ROWS).astype(jnp.int32)
    lower_panels = centred(splits[2], (ROWS, INNER), INNER ** -0.5, 0.125, ((0, 128), (1, 8)))
    upper_rows = centred(splits[3], (SLAB, INNER), 1.0, 6.0, ((0, 128), (1, 8)))
    return dict(slab_cols=slab_cols, pivots=pivots, lower_panels=lower_panels, upper_rows=upper_rows)


def reference(slab_cols, pivots, lower_panels, upper_rows):
    permuted = jnp.take(slab_cols, pivots.astype(jnp.int32), axis=1)
    update = lax.dot_general(upper_rows, lower_panels, (((1,), (1,)), ((), ())), preferred_element_type=jnp.float32)
    return permuted - update
```

```python
import jax
import jax.numpy as jnp
from jax import lax
from jax.sharding import Mesh, PartitionSpec as P

BULK = ("x", "yh", "yl", "zh")
OWNER = ("zl", "c")
AXES = {"x": 8, "yh": 4, "yl": 2, "zh": 2, "zl": 4, "c": 2}


def gather(block, axes):
    members = lax.axis_size(axes)
    copies = jnp.broadcast_to(block[None], (members,) + block.shape)
    return lax.all_to_all(copies, axes, 0, 0, tiled=True)


def shards(slab_cols, pivots, lower_panels, upper_rows):
    owner_index = lax.axis_index(OWNER)
    row_block = slab_cols.shape[1]
    columns, inner = upper_rows.shape

    slab = lax.all_gather(slab_cols, OWNER, axis=1, tiled=True)

    upper = gather(upper_rows, ("yh", "zh")).reshape(-1, inner)
    lower = gather(lower_panels, ("x", "yl"))

    core = lax.axis_index("c")
    lower = lower.reshape(4, 2, -1, inner)

    def partial_value(parity):
        rows = lax.dynamic_index_in_dim(lower, parity, axis=1, keepdims=False)
        dots = [
            lax.dot_general(upper, rows[z], (((1,), (1,)), ((), ())), preferred_element_type=jnp.float32)
            for z in range(4)
        ]
        return jnp.stack(dots)

    kept = lax.ppermute(partial_value(1 - core), "c", [(0, 1), (1, 0)]) + partial_value(core)

    pieces = kept.reshape(32, columns, -1)
    pieces = lax.all_to_all(pieces, ("zl", "yh", "zh"), 0, 0, tiled=True)
    pieces = pieces.reshape(4, 4, 2, columns, 2, -1).sum(0)
    update = pieces.transpose(2, 0, 3, 1, 4).reshape(columns, row_block)

    local_pivots = lax.dynamic_slice_in_dim(pivots, owner_index * row_block, row_block)
    return jnp.take(slab, local_pivots, axis=1, mode="clip") - update


def solution(mesh):
    fine = Mesh(mesh.devices.reshape(tuple(AXES.values())), tuple(AXES))
    spec = P(BULK, OWNER)
    return jax.shard_map(
        shards, mesh=fine, in_specs=(spec, P(), spec, spec), out_specs=spec, check_vma=False
    )
```

```python
import jax
import jax.numpy as jnp
from jax import lax
from jax.experimental import pallas as pl
from jax.experimental.pallas import tpu as pltpu
from jax.sharding import Mesh, PartitionSpec as P


BULK = ("x", "yh", "yl", "zh")
OWNER = ("zl", "c")
AXES = {"x": 8, "yh": 4, "yl": 2, "zh": 2, "zl": 4, "c": 2}
SWAP = [(0, 1), (1, 0)]
VMEM = pl.BlockSpec(memory_space=pltpu.VMEM)
SMEM = pl.BlockSpec(memory_space=pltpu.SMEM)


def gather(block, axes):
    members = lax.axis_size(axes)
    copies = jnp.broadcast_to(block[None], (members,) + block.shape)
    return lax.all_to_all(copies, axes, 0, 0, tiled=True)


def product(parity_ref, upper_ref, lower_ref, out_ref):
    upper = upper_ref[...]
    for z in range(4):
        out_ref[z] = lax.dot_general(
            upper, lower_ref[2 * z + parity_ref[0]], (((1,), (1,)), ((), ())), preferred_element_type=jnp.float32
        )


def permute(place_ref, pivots_ref, own_ref, other_ref, out_ref):
    owner, core = place_ref[0], place_ref[1]

    def block(b, _):
        index = pivots_ref[pl.ds(owner * 8 + b, 1), :]
        side = ((index >> 10) & 1) ^ core
        key = jnp.broadcast_to(side * 32 + (index >> 11) * 8 + ((index >> 7) & 7), (32, 128))
        lane = jnp.broadcast_to(index & 127, (32, 128))
        found = jnp.zeros((32, 128), jnp.float32)
        for k in range(64):
            ref = own_ref if k < 32 else other_ref
            source = ref[(k % 32) // 8, :, (k % 8) * 128 : (k % 8 + 1) * 128]
            found = jnp.where(key == k, jnp.take_along_axis(source, lane, axis=1, mode="promise_in_bounds"), found)
        out_ref[:, pl.ds(pl.multiple_of(b * 128, 128), 128)] = found
        return 0

    lax.fori_loop(0, 8, block, 0)


def finish(pieces_ref, permuted_ref, out_ref):
    low = lax.broadcasted_iota(jnp.int32, (32, 128), 1) < 64
    for yh in range(4):
        first, second = (sum(pieces_ref[zl * 8 + yh * 2 + zh] for zl in range(4)) for zh in range(2))
        blocks = (
            jnp.where(low, first, pltpu.roll(second, 64, 1)),
            jnp.where(low, pltpu.roll(first, 64, 1), second),
        )
        for yl in range(2):
            at = slice((yh * 2 + yl) * 128, (yh * 2 + yl + 1) * 128)
            out_ref[:, at] = permuted_ref[:, at] - blocks[yl]


def shards(slab_cols, pivots, lower_panels, upper_rows):
    core = lax.axis_index("c")
    columns, row_block = slab_cols.shape
    inner = upper_rows.shape[1]

    upper = gather(upper_rows, ("yh", "zh")).reshape(-1, inner)
    lower = gather(lower_panels, ("x", "yl")).reshape(8, -1, inner)

    own = lax.all_gather(slab_cols, "zl", axis=0)
    other = lax.ppermute(own, "c", SWAP)

    def partial_value(parity):
        return pl.pallas_call(
            product,
            out_shape=jax.ShapeDtypeStruct((4, upper.shape[0], lower.shape[1]), jnp.float32),
            in_specs=[SMEM, VMEM, VMEM],
            out_specs=VMEM,
            name="product",
        )(parity.reshape(1), upper, lower)

    kept = lax.ppermute(partial_value(1 - core), "c", SWAP) + partial_value(core)

    pieces = lax.all_to_all(kept.reshape(32, columns, -1), ("zl", "yh", "zh"), 0, 0, tiled=True)

    permuted = pl.pallas_call(
        permute,
        out_shape=jax.ShapeDtypeStruct((columns, row_block), jnp.float32),
        in_specs=[SMEM, VMEM, VMEM, VMEM],
        out_specs=VMEM,
        name="permute",
    )(jnp.stack([lax.axis_index(OWNER), core]), pivots.reshape(-1, 128), own, other)
    return pl.pallas_call(
        finish,
        out_shape=jax.ShapeDtypeStruct((columns, row_block), jnp.float32),
        in_specs=[VMEM, VMEM],
        out_specs=VMEM,
        name="finish",
    )(pieces, permuted)


def solution(mesh):
    fine = Mesh(mesh.devices.reshape(tuple(AXES.values())), tuple(AXES))
    spec = P(BULK, OWNER)

    return jax.shard_map(shards, mesh=fine, in_specs=(spec, P(), spec, spec), out_specs=spec, check_vma=False)
```

```python
import jax
import jax.numpy as jnp
from jax import lax
from jax.experimental import pallas as pl
from jax.experimental.pallas import tpu as pltpu
from jax.sharding import Mesh, PartitionSpec as P


BULK = ("x", "yh", "yl", "zh")
OWNER = ("zl", "c")
AXES = {"x": 8, "yh": 4, "yl": 2, "zh": 2, "zl": 4, "c": 2}
SWAP = [(0, 1), (1, 0)]
VMEM = pl.BlockSpec(memory_space=pltpu.VMEM)
SMEM = pl.BlockSpec(memory_space=pltpu.SMEM)


def kernel(body, scalars, arrays, out, vmem_out=True):
    arrays = [pltpu.with_memory_space_constraint(a, pltpu.VMEM) for a in arrays]
    return pl.pallas_call(
        body,
        out_shape=pltpu.VMEM(out, jnp.float32) if vmem_out else jax.ShapeDtypeStruct(out, jnp.float32),
        in_specs=[SMEM] * len(scalars) + [VMEM] * len(arrays),
        out_specs=VMEM,
    )(*scalars, *arrays)


def gather(block, axes):
    members = lax.axis_size(axes)
    copies = jnp.broadcast_to(block[None], (members,) + block.shape)
    return lax.all_to_all(copies, axes, 0, 0, tiled=True)


def product(parity_ref, upper_ref, lower_ref, out_ref):
    upper = upper_ref[...]
    for z in range(4):
        out_ref[z] = lax.dot_general(
            upper, lower_ref[2 * z + parity_ref[0]], (((1,), (1,)), ((), ())), preferred_element_type=jnp.float32
        )


def add(left_ref, right_ref, out_ref):
    out_ref[...] = left_ref[...] + right_ref[...]


def permute(place_ref, pivots_ref, own_ref, other_ref, out_ref):
    owner, core = place_ref[0], place_ref[1]

    def block(b, _):
        index = pivots_ref[pl.ds(owner * 8 + b, 1), :]
        side = ((index >> 10) & 1) ^ core
        key = jnp.broadcast_to(side * 32 + (index >> 11) * 8 + ((index >> 7) & 7), (32, 128))
        lane = jnp.broadcast_to(index & 127, (32, 128))
        found = jnp.zeros((32, 128), jnp.float32)
        for k in range(64):
            ref = own_ref if k < 32 else other_ref
            source = ref[(k % 32) // 8, :, (k % 8) * 128 : (k % 8 + 1) * 128]
            found = jnp.where(key == k, jnp.take_along_axis(source, lane, axis=1, mode="promise_in_bounds"), found)
        out_ref[:, pl.ds(pl.multiple_of(b * 128, 128), 128)] = found
        return 0

    lax.fori_loop(0, 8, block, 0)


def finish(pieces_ref, permuted_ref, out_ref):
    low = lax.broadcasted_iota(jnp.int32, (32, 128), 1) < 64
    for yh in range(4):
        first, second = (sum(pieces_ref[zl * 8 + yh * 2 + zh] for zl in range(4)) for zh in range(2))
        blocks = (
            jnp.where(low, first, pltpu.roll(second, 64, 1)),
            jnp.where(low, pltpu.roll(first, 64, 1), second),
        )
        for yl in range(2):
            at = slice((yh * 2 + yl) * 128, (yh * 2 + yl + 1) * 128)
            out_ref[:, at] = permuted_ref[:, at] - blocks[yl]


def shards(slab_cols, pivots, lower_panels, upper_rows):
    core = lax.axis_index("c")
    columns, row_block = slab_cols.shape
    inner = upper_rows.shape[1]

    upper = gather(upper_rows, ("yh", "zh")).reshape(-1, inner)
    lower = gather(lower_panels, ("x", "yl")).reshape(8, -1, inner)

    own = lax.all_gather(slab_cols, "zl", axis=0)
    other = lax.ppermute(own, "c", SWAP)

    def partial_value(parity):
        out = (4, upper.shape[0], lower.shape[1])
        return kernel(product, [parity.reshape(1)], [upper, lower], out)

    received = lax.ppermute(partial_value(1 - core), "c", SWAP)
    kept = partial_value(core)
    kept = kernel(add, [], [received, kept], kept.shape)

    pieces = lax.all_to_all(kept.reshape(32, columns, -1), ("zl", "yh", "zh"), 0, 0, tiled=True)

    place = jnp.stack([lax.axis_index(OWNER), core])
    permuted = kernel(permute, [place], [pivots.reshape(-1, 128), own, other], (columns, row_block))
    return kernel(finish, [], [pieces, permuted], (columns, row_block), vmem_out=False)


def solution(mesh):
    fine = Mesh(mesh.devices.reshape(tuple(AXES.values())), tuple(AXES))
    spec = P(BULK, OWNER)

    return jax.shard_map(shards, mesh=fine, in_specs=(spec, P(), spec, spec), out_specs=spec, check_vma=False)
```

```python
import jax
import jax.numpy as jnp
from jax import lax
from jax.experimental import pallas as pl
from jax.experimental.pallas import tpu as pltpu
from jax.sharding import Mesh, PartitionSpec as P


BULK = ("x", "yh", "yl", "zh")
OWNER = ("z1", "z0", "c")
AXES = {"x": 8, "yh": 4, "yl": 2, "zh": 2, "z1": 2, "z0": 2, "c": 2}
SWAP = [(0, 1), (1, 0)]
VMEM = pl.BlockSpec(memory_space=pltpu.VMEM)
SMEM = pl.BlockSpec(memory_space=pltpu.SMEM)


def kernel(body, scalars, arrays, out, vmem_out=True):
    arrays = [pltpu.with_memory_space_constraint(a, pltpu.VMEM) for a in arrays]
    return pl.pallas_call(
        body,
        out_shape=pltpu.VMEM(out, jnp.float32) if vmem_out else jax.ShapeDtypeStruct(out, jnp.float32),
        in_specs=[SMEM] * len(scalars) + [VMEM] * len(arrays),
        out_specs=VMEM,
    )(*scalars, *arrays)


def product(parity_ref, upper_ref, lower_ref, out_ref):
    for z in range(4):
        halves = []
        for half in range(2):
            dots = [
                lax.dot_general(
                    upper_ref[:, z0, half * 16 : half * 16 + 16, :].reshape(128, 256),
                    lower_ref[2 * z + parity_ref[0], z0],
                    (((1,), (1,)), ((), ())),
                    preferred_element_type=jnp.float32,
                )
                for z0 in range(2)
            ]
            halves.append(dots[0] + dots[1])
        out_ref[z] = jnp.concatenate(halves, axis=1).reshape(8, 16, 128)


def add(left_ref, right_ref, out_ref):
    out_ref[...] = left_ref[...] + right_ref[...]


def permute(place_ref, pivots_ref, own_ref, other_ref, out_ref):
    owner, core = place_ref[0], place_ref[1]

    def block(b, _):
        index = pivots_ref[pl.ds(owner * 8 + b, 1), :]
        side = ((index >> 10) & 1) ^ core
        key = jnp.broadcast_to(side * 32 + (index >> 11) * 8 + ((index >> 7) & 7), (32, 128))
        lane = jnp.broadcast_to(index & 127, (32, 128))
        found = jnp.zeros((32, 128), jnp.float32)
        for k in range(64):
            ref = own_ref if k < 32 else other_ref
            source = ref[(k % 32) // 8, :, (k % 8) * 128 : (k % 8 + 1) * 128]
            found = jnp.where(key == k, jnp.take_along_axis(source, lane, axis=1, mode="promise_in_bounds"), found)
        out_ref[:, pl.ds(pl.multiple_of(b * 128, 128), 128)] = found
        return 0

    lax.fori_loop(0, 8, block, 0)


def finish(pieces_ref, permuted_ref, out_ref):
    quarter = lax.broadcasted_iota(jnp.int32, (16, 128), 1) // 32
    for yh in range(4):
        sums = [pieces_ref[0, q % 2, yh, q // 2] + pieces_ref[1, q % 2, yh, q // 2] for q in range(4)]
        for yl in range(2):
            at = slice((yh * 2 + yl) * 128, (yh * 2 + yl + 1) * 128)
            for half in range(2):
                rows = slice(half * 16, half * 16 + 16)
                update = sums[0]
                for q in range(4):
                    shift = (q * 32 - half * 64 - yl * 32) % 128
                    moved = pltpu.roll(sums[q], shift, 1) if shift else sums[q]
                    update = jnp.where(quarter == q, moved, update)
                out_ref[rows, at] = permuted_ref[rows, at] - update


def shards(slab_cols, pivots, lower_panels, upper_rows):
    core = lax.axis_index("c")
    columns, row_block = slab_cols.shape
    inner = upper_rows.shape[1]

    upper = jnp.broadcast_to(upper_rows[None], (16, columns, inner))
    upper = lax.all_to_all(upper, ("yh", "zh", "z0"), 0, 0, tiled=True).reshape(8, 2, columns, inner)
    lower = jnp.broadcast_to(lower_panels.reshape(1, 2, 1, -1, inner), (8, 2, 2, 32, inner))
    lower = lax.all_to_all(lower.reshape(32, 32, inner), ("x", "z0", "yl"), 0, 0, tiled=True)
    lower = lower.reshape(8, 2, 64, inner)

    own = lax.all_gather(slab_cols, ("z1", "z0"), axis=0)
    other = lax.ppermute(own, "c", SWAP)

    def partial_value(parity):
        out = (4, 8, 16, 128)
        return kernel(product, [parity.reshape(1)], [upper, lower], out)

    received = lax.ppermute(partial_value(1 - core), "c", SWAP)
    kept = partial_value(core)
    kept = kernel(add, [], [received, kept], kept.shape)

    pieces = lax.all_to_all(kept.reshape(32, 16, 128), ("z1", "z0", "yh", "zh"), 0, 0, tiled=True)
    pieces = pieces.reshape(2, 2, 4, 2, 16, 128)

    place = jnp.stack([lax.axis_index(OWNER), core])
    permuted = kernel(permute, [place], [pivots.reshape(-1, 128), own, other], (columns, row_block))
    return kernel(finish, [], [pieces, permuted], (columns, row_block), vmem_out=False)


def solution(mesh):
    fine = Mesh(mesh.devices.reshape(tuple(AXES.values())), tuple(AXES))
    spec = P(BULK, OWNER)

    return jax.shard_map(shards, mesh=fine, in_specs=(spec, P(), spec, spec), out_specs=spec, check_vma=False)
```

```python
import jax
import jax.numpy as jnp
from jax import lax
from jax.experimental import pallas as pl
from jax.experimental.pallas import tpu as pltpu
from jax.sharding import Mesh, PartitionSpec as P


BULK = ("x", "y", "zh")
OWNER = ("zl", "c")
AXES = {"x": 8, "y": 8, "zh": 2, "zl": 4, "c": 2}
SWAP = [(0, 1), (1, 0)]
VMEM = pl.BlockSpec(memory_space=pltpu.VMEM)
SMEM = pl.BlockSpec(memory_space=pltpu.SMEM)


def kernel(body, scalars, arrays, out, dtype=jnp.float32, vmem_out=True):
    arrays = [pltpu.with_memory_space_constraint(a, pltpu.VMEM) for a in arrays]
    return pl.pallas_call(
        body,
        out_shape=pltpu.VMEM(out, dtype) if vmem_out else jax.ShapeDtypeStruct(out, dtype),
        in_specs=[SMEM] * len(scalars) + [VMEM] * len(arrays),
        out_specs=VMEM,
    )(*scalars, *arrays)


def copies(own_ref, other_ref, out_ref):
    for x in range(8):
        out_ref[x, 0] = own_ref[...]
        out_ref[x, 1] = other_ref[...]


def product(place_ref, upper_ref, lower_ref, out_ref):
    parity, zh = place_ref[0], place_ref[1]
    for z in range(4):
        owner = 2 * z + parity
        rows = jnp.concatenate([lower_ref[owner, zh], lower_ref[owner, 1 - zh]], axis=0)
        out_ref[z] = lax.dot_general(
            upper_ref[...], rows, (((1,), (1,)), ((), ())), preferred_element_type=jnp.float32
        )


def add(left_ref, right_ref, out_ref):
    out_ref[...] = left_ref[...] + right_ref[...]


def permute(place_ref, pivots_ref, own_ref, other_ref, out_ref):
    owner, core = place_ref[0], place_ref[1]

    def block(b, _):
        index = pivots_ref[pl.ds(owner * 8 + b, 1), :]
        side = ((index >> 10) & 1) ^ core
        key = jnp.broadcast_to(side * 32 + (index >> 11) * 8 + ((index >> 7) & 7), (32, 128))
        lane = jnp.broadcast_to(index & 127, (32, 128))
        found = jnp.zeros((32, 128), jnp.float32)
        for k in range(64):
            ref = own_ref if k < 32 else other_ref
            source = ref[(k % 32) // 8, :, (k % 8) * 128 : (k % 8 + 1) * 128]
            found = jnp.where(key == k, jnp.take_along_axis(source, lane, axis=1, mode="promise_in_bounds"), found)
        out_ref[:, pl.ds(pl.multiple_of(b * 128, 128), 128)] = found
        return 0

    lax.fori_loop(0, 8, block, 0)


def finish(pieces_ref, permuted_ref, out_ref):
    for y in range(8):
        at = slice(y * 128, (y + 1) * 128)
        out_ref[:, at] = permuted_ref[:, at] - sum(pieces_ref[zl * 8 + y] for zl in range(4))


def shards(slab_cols, pivots, lower_panels, upper_rows):
    core = lax.axis_index("c")
    columns, row_block = slab_cols.shape
    inner = upper_rows.shape[1]

    upper = jnp.broadcast_to(upper_rows[None], (8, columns, inner))
    upper = lax.all_to_all(upper, "y", 0, 0, tiled=True).reshape(-1, inner)
    paired = lax.ppermute(lower_panels, "zh", SWAP)
    lower = kernel(copies, [], [lower_panels, paired], (8, 2, 64, inner), dtype=jnp.bfloat16)
    lower = lax.all_to_all(lower.reshape(8, 128, inner), "x", 0, 0, tiled=True).reshape(8, 2, 64, inner)

    own = lax.all_gather(slab_cols, "zl", axis=0)
    other = lax.ppermute(own, "c", SWAP)

    def partial_value(parity):
        place = jnp.stack([parity, lax.axis_index("zh")])
        return kernel(product, [place], [upper, lower], (4, 256, 128))

    received = lax.ppermute(partial_value(1 - core), "c", SWAP)
    kept = kernel(add, [], [received, partial_value(core)], (4, 256, 128))

    pieces = lax.all_to_all(kept.reshape(32, columns, -1), ("zl", "y"), 0, 0, tiled=True)

    place = jnp.stack([lax.axis_index(OWNER), core])
    permuted = kernel(permute, [place], [pivots.reshape(-1, 128), own, other], (columns, row_block))
    return kernel(finish, [], [pieces, permuted], (columns, row_block), vmem_out=False)


def solution(mesh):
    fine = Mesh(mesh.devices.reshape(tuple(AXES.values())), tuple(AXES))
    spec = P(BULK, OWNER)

    return jax.shard_map(shards, mesh=fine, in_specs=(spec, P(), spec, spec), out_specs=spec, check_vma=False)
```

```python
import jax
import jax.numpy as jnp
from jax import lax
from jax.experimental import pallas as pl
from jax.experimental.pallas import tpu as pltpu
from jax.sharding import Mesh, PartitionSpec as P


BULK = ("x", "y", "zh")
OWNER = ("zl", "c")
AXES = {"x": 8, "y": 8, "zh": 2, "zl": 4, "c": 2}
SWAP = [(0, 1), (1, 0)]
VMEM = pl.BlockSpec(memory_space=pltpu.VMEM)
SMEM = pl.BlockSpec(memory_space=pltpu.SMEM)


def kernel(body, scalars, arrays, out, dtype=jnp.float32, vmem_out=True):
    arrays = [pltpu.with_memory_space_constraint(a, pltpu.VMEM) for a in arrays]
    return pl.pallas_call(
        body,
        out_shape=pltpu.VMEM(out, dtype) if vmem_out else jax.ShapeDtypeStruct(out, dtype),
        in_specs=[SMEM] * len(scalars) + [VMEM] * len(arrays),
        out_specs=VMEM,
    )(*scalars, *arrays)


def copies(zh_ref, own_ref, other_ref, out_ref):
    zh = zh_ref[0]
    for x in range(8):
        out_ref[x, zh] = own_ref[...]
        out_ref[x, 1 - zh] = other_ref[...]


def product(parity_ref, upper_ref, lower_ref, out_ref):
    upper = upper_ref[...]
    for z in range(4):
        out_ref[z] = lax.dot_general(
            upper, lower_ref[2 * z + parity_ref[0]], (((1,), (1,)), ((), ())), preferred_element_type=jnp.float32
        )


def add(left_ref, right_ref, out_ref):
    out_ref[...] = left_ref[...] + right_ref[...]


def permute(owner_ref, core_ref, pivots_ref, own_ref, other_ref, out_ref):
    owner, core = owner_ref[0], core_ref[0]

    def block(b, _):
        index = pivots_ref[pl.ds(owner * 8 + b, 1), :]
        side = ((index >> 10) & 1) ^ core
        key = jnp.broadcast_to(side * 32 + (index >> 11) * 8 + ((index >> 7) & 7), (32, 128))
        lane = jnp.broadcast_to(index & 127, (32, 128))
        found = jnp.zeros((32, 128), jnp.float32)
        for k in range(64):
            ref = own_ref if k < 32 else other_ref
            source = ref[(k % 32) // 8, :, (k % 8) * 128 : (k % 8 + 1) * 128]
            found = jnp.where(key == k, jnp.take_along_axis(source, lane, axis=1, mode="promise_in_bounds"), found)
        out_ref[:, pl.ds(pl.multiple_of(b * 128, 128), 128)] = found
        return 0

    lax.fori_loop(0, 8, block, 0)


def finish(pieces_ref, permuted_ref, out_ref):
    for y in range(8):
        at = slice(y * 128, (y + 1) * 128)
        out_ref[:, at] = permuted_ref[:, at] - sum(pieces_ref[zl * 8 + y] for zl in range(4))


def shards(slab_cols, pivots, lower_panels, upper_rows):
    core, zh, owner = (lax.axis_index(axes).reshape(1) for axes in ("c", "zh", OWNER))
    columns, row_block = slab_cols.shape
    inner = upper_rows.shape[1]

    upper = jnp.broadcast_to(upper_rows[None], (8, columns, inner))
    upper = lax.all_to_all(upper, "y", 0, 0, tiled=True).reshape(-1, inner)
    paired = lax.ppermute(lower_panels, "zh", SWAP)
    lower = kernel(copies, [zh], [lower_panels, paired], (8, 2, 64, inner), dtype=jnp.bfloat16)
    lower = lax.all_to_all(lower.reshape(8, 128, inner), "x", 0, 0, tiled=True)

    own = lax.all_gather(slab_cols, "zl", axis=0)
    other = lax.ppermute(own, "c", SWAP)

    def partial_value(parity):
        return kernel(product, [parity], [upper, lower], (4, 256, 128))

    received = lax.ppermute(partial_value(1 - core), "c", SWAP)
    kept = kernel(add, [], [received, partial_value(core)], (4, 256, 128))

    pieces = lax.all_to_all(kept.reshape(32, columns, -1), ("zl", "y"), 0, 0, tiled=True)

    permuted = kernel(permute, [owner, core], [pivots.reshape(-1, 128), own, other], (columns, row_block))
    return kernel(finish, [], [pieces, permuted], (columns, row_block), vmem_out=False)


def solution(mesh):
    fine = Mesh(mesh.devices.reshape(tuple(AXES.values())), tuple(AXES))
    spec = P(BULK, OWNER)

    return jax.shard_map(shards, mesh=fine, in_specs=(spec, P(), spec, spec), out_specs=spec, check_vma=False)
```

```python
import jax
import jax.numpy as jnp
from jax import lax
from jax.experimental import pallas as pl
from jax.experimental.pallas import tpu as pltpu
from jax.sharding import Mesh, PartitionSpec as P


BULK = ("x", "y", "zh")
OWNER = ("z1", "z0", "c")
AXES = {"x": 8, "y": 8, "zh": 2, "z1": 2, "z0": 2, "c": 2}
SWAP = [(0, 1), (1, 0)]
VMEM = pl.BlockSpec(memory_space=pltpu.VMEM)
SMEM = pl.BlockSpec(memory_space=pltpu.SMEM)


def kernel(body, scalars, arrays, out, dtype=jnp.float32, vmem_out=True):
    arrays = [pltpu.with_memory_space_constraint(a, pltpu.VMEM) for a in arrays]
    return pl.pallas_call(
        body,
        out_shape=pltpu.VMEM(out, dtype) if vmem_out else jax.ShapeDtypeStruct(out, dtype),
        in_specs=[SMEM] * len(scalars) + [VMEM] * len(arrays),
        out_specs=VMEM,
    )(*scalars, *arrays)


def copies(zh_ref, own_ref, other_ref, out_ref):
    zh = zh_ref[0]
    for x in range(8):
        out_ref[x, zh] = own_ref[...]
        out_ref[x, 1 - zh] = other_ref[...]


def repeat(block_ref, out_ref):
    for y in range(8):
        out_ref[y] = block_ref[...]


def line(z0_ref, z1_ref, own_ref, near_ref, far_ref, far_near_ref, out_ref):
    z0, z1 = z0_ref[0], z1_ref[0]
    out_ref[2 * z1 + z0] = own_ref[...]
    out_ref[2 * z1 + 1 - z0] = near_ref[...]
    out_ref[2 * (1 - z1) + z0] = far_ref[...]
    out_ref[2 * (1 - z1) + 1 - z0] = far_near_ref[...]


def product(parity_ref, upper_ref, lower_ref, out_ref):
    upper = upper_ref[...]
    for z in range(4):
        out_ref[z] = lax.dot_general(
            upper, lower_ref[2 * z + parity_ref[0]], (((1,), (1,)), ((), ())), preferred_element_type=jnp.float32
        )


def add(left_ref, right_ref, out_ref):
    out_ref[...] = left_ref[...] + right_ref[...]


def places(owner_ref, core_ref, pivots_ref, out_ref):
    index = pivots_ref[pl.ds(pl.multiple_of(owner_ref[0] * 8, 8), 8), :]
    side = ((index >> 10) & 1) ^ core_ref[0]
    out_ref[0] = index & 127
    out_ref[1] = side * 32 + (index >> 11) * 8 + ((index >> 7) & 7)


def permute(places_ref, own_ref, other_ref, out_ref):
    def block(b, _):
        lane = jnp.broadcast_to(places_ref[0, pl.ds(b, 1), :], (32, 128))
        key = jnp.broadcast_to(places_ref[1, pl.ds(b, 1), :], (32, 128))
        found = jnp.zeros((32, 128), jnp.float32)
        for k in range(64):
            ref = own_ref if k < 32 else other_ref
            source = ref[(k % 32) // 8, :, (k % 8) * 128 : (k % 8 + 1) * 128]
            found = jnp.where(key == k, jnp.take_along_axis(source, lane, axis=1, mode="promise_in_bounds"), found)
        out_ref[:, pl.ds(pl.multiple_of(b * 128, 128), 128)] = found
        return 0

    lax.fori_loop(0, 8, block, 0)


def finish(pieces_ref, permuted_ref, out_ref):
    for y in range(8):
        at = slice(y * 128, (y + 1) * 128)
        out_ref[:, at] = permuted_ref[:, at] - sum(pieces_ref[zl * 8 + y] for zl in range(4))


def shards(slab_cols, pivots, lower_panels, upper_rows):
    core, zh, owner = (lax.axis_index(axes).reshape(1) for axes in ("c", "zh", OWNER))
    z0, z1 = (lax.axis_index(axis).reshape(1) for axis in ("z0", "z1"))
    columns, row_block = slab_cols.shape
    inner = upper_rows.shape[1]

    upper = kernel(repeat, [], [upper_rows], (8, columns, inner), dtype=jnp.bfloat16)
    upper = lax.all_to_all(upper, "y", 0, 0, tiled=True).reshape(-1, inner)
    paired = lax.ppermute(lower_panels, "zh", SWAP)
    lower = kernel(copies, [zh], [lower_panels, paired], (8, 2, 64, inner), dtype=jnp.bfloat16)
    lower = lax.all_to_all(lower.reshape(8, 128, inner), "x", 0, 0, tiled=True)

    near = lax.ppermute(slab_cols, "z0", SWAP)
    far = lax.ppermute(slab_cols, "z1", SWAP)
    far_near = lax.ppermute(near, "z1", SWAP)
    own = kernel(line, [z0, z1], [slab_cols, near, far, far_near], (4, columns, row_block))
    other = lax.ppermute(own, "c", SWAP)

    def partial_value(parity):
        return kernel(product, [parity], [upper, lower], (4, 256, 128))

    received = lax.ppermute(partial_value(1 - core), "c", SWAP)
    kept = kernel(add, [], [received, partial_value(core)], (4, 256, 128))

    pieces = lax.all_to_all(kept.reshape(32, columns, -1), ("z1", "z0", "y"), 0, 0, tiled=True)

    at = kernel(places, [owner, core], [pivots.reshape(-1, 128)], (2, 8, 128), dtype=jnp.int32)
    permuted = kernel(permute, [], [at, own, other], (columns, row_block))
    return kernel(finish, [], [pieces, permuted], (columns, row_block), vmem_out=False)


def solution(mesh):
    fine = Mesh(mesh.devices.reshape(tuple(AXES.values())), tuple(AXES))
    spec = P(BULK, OWNER)

    return jax.shard_map(shards, mesh=fine, in_specs=(spec, P(), spec, spec), out_specs=spec, check_vma=False)
```

```python
import jax
import jax.numpy as jnp
from jax import lax
from jax.experimental import pallas as pl
from jax.experimental.pallas import tpu as pltpu
from jax.sharding import Mesh, PartitionSpec as P


BULK = ("x", "y", "zh")
OWNER = ("z1", "z0", "c")
AXES = {"x": 8, "y": 8, "zh": 2, "z1": 2, "z0": 2, "c": 2}
SWAP = [(0, 1), (1, 0)]
VMEM = pl.BlockSpec(memory_space=pltpu.VMEM)
SMEM = pl.BlockSpec(memory_space=pltpu.SMEM)


def kernel(body, scalars, arrays, out, dtype=jnp.float32, vmem_out=True):
    arrays = [pltpu.with_memory_space_constraint(a, pltpu.VMEM) for a in arrays]
    return pl.pallas_call(
        body,
        out_shape=pltpu.VMEM(out, dtype) if vmem_out else jax.ShapeDtypeStruct(out, dtype),
        in_specs=[SMEM] * len(scalars) + [VMEM] * len(arrays),
        out_specs=VMEM,
    )(*scalars, *arrays)


def copies(zh_ref, own_ref, other_ref, out_ref):
    zh = zh_ref[0]
    for x in range(8):
        for z0 in range(2):
            rows = slice(z0 * 32, z0 * 32 + 32)
            out_ref[x, z0, zh] = own_ref[rows]
            out_ref[x, z0, 1 - zh] = other_ref[rows]


def repeat(block_ref, out_ref):
    for y in range(16):
        out_ref[y] = block_ref[...]


def line(z0_ref, z1_ref, own_ref, near_ref, far_ref, far_near_ref, out_ref):
    z0, z1 = z0_ref[0], z1_ref[0]
    out_ref[2 * z1 + z0] = own_ref[...]
    out_ref[2 * z1 + 1 - z0] = near_ref[...]
    out_ref[2 * (1 - z1) + z0] = far_ref[...]
    out_ref[2 * (1 - z1) + 1 - z0] = far_near_ref[...]


def product(parity_ref, upper_ref, lower_ref, out_ref):
    for z in range(4):
        halves = []
        for half in range(2):
            dots = [
                lax.dot_general(
                    upper_ref[:, z0, half * 16 : half * 16 + 16, :].reshape(128, 256),
                    lower_ref[2 * z + parity_ref[0], z0],
                    (((1,), (1,)), ((), ())),
                    preferred_element_type=jnp.float32,
                )
                for z0 in range(2)
            ]
            halves.append(dots[0] + dots[1])
        out_ref[z] = jnp.concatenate(halves, axis=1).reshape(8, 16, 128)


def add(left_ref, right_ref, out_ref):
    out_ref[...] = left_ref[...] + right_ref[...]


def places(owner_ref, core_ref, pivots_ref, out_ref):
    index = pivots_ref[pl.ds(pl.multiple_of(owner_ref[0] * 8, 8), 8), :]
    side = ((index >> 10) & 1) ^ core_ref[0]
    out_ref[0] = index & 127
    out_ref[1] = side * 32 + (index >> 11) * 8 + ((index >> 7) & 7)


def permute(places_ref, own_ref, other_ref, out_ref):
    def block(b, _):
        lane = jnp.broadcast_to(places_ref[0, pl.ds(b, 1), :], (32, 128))
        key = jnp.broadcast_to(places_ref[1, pl.ds(b, 1), :], (32, 128))
        found = jnp.zeros((32, 128), jnp.float32)
        for k in range(64):
            ref = own_ref if k < 32 else other_ref
            source = ref[(k % 32) // 8, :, (k % 8) * 128 : (k % 8 + 1) * 128]
            found = jnp.where(key == k, jnp.take_along_axis(source, lane, axis=1, mode="promise_in_bounds"), found)
        out_ref[:, pl.ds(pl.multiple_of(b * 128, 128), 128)] = found
        return 0

    lax.fori_loop(0, 8, block, 0)


def finish(pieces_ref, permuted_ref, out_ref):
    quarter = lax.broadcasted_iota(jnp.int32, (16, 128), 1) // 32
    for y in range(8):
        at = slice(y * 128, (y + 1) * 128)
        sums = [pieces_ref[0, z0, y] + pieces_ref[1, z0, y] for z0 in range(2)]
        for half in range(2):
            rows = slice(half * 16, half * 16 + 16)
            update = sums[0]
            for q in range(4):
                zh, z0 = q // 2, q % 2
                shift = (q * 32 - half * 64 - zh * 32) % 128
                moved = pltpu.roll(sums[z0], shift, 1) if shift else sums[z0]
                update = jnp.where(quarter == q, moved, update)
            out_ref[rows, at] = permuted_ref[rows, at] - update


def shards(slab_cols, pivots, lower_panels, upper_rows):
    core, zh, owner = (lax.axis_index(axes).reshape(1) for axes in ("c", "zh", OWNER))
    z0, z1 = (lax.axis_index(axis).reshape(1) for axis in ("z0", "z1"))
    columns, row_block = slab_cols.shape
    inner = upper_rows.shape[1]

    upper = kernel(repeat, [], [upper_rows], (16, columns, inner), dtype=jnp.bfloat16)
    upper = lax.all_to_all(upper, ("y", "z0"), 0, 0, tiled=True).reshape(8, 2, columns, inner)
    paired = lax.ppermute(lower_panels, "zh", SWAP)
    lower = kernel(copies, [zh], [lower_panels, paired], (8, 2, 2, 32, inner), dtype=jnp.bfloat16)
    lower = lax.all_to_all(lower.reshape(16, 64, inner), ("x", "z0"), 0, 0, tiled=True).reshape(8, 2, 64, inner)

    near = lax.ppermute(slab_cols, "z0", SWAP)
    far = lax.ppermute(slab_cols, "z1", SWAP)
    far_near = lax.ppermute(near, "z1", SWAP)
    own = kernel(line, [z0, z1], [slab_cols, near, far, far_near], (4, columns, row_block))
    other = lax.ppermute(own, "c", SWAP)

    def partial_value(parity):
        return kernel(product, [parity], [upper, lower], (4, 8, 16, 128))

    received = lax.ppermute(partial_value(1 - core), "c", SWAP)
    kept = kernel(add, [], [received, partial_value(core)], (4, 8, 16, 128))

    pieces = lax.all_to_all(kept.reshape(32, 16, 128), ("z1", "z0", "y"), 0, 0, tiled=True)
    pieces = pieces.reshape(2, 2, 8, 16, 128)

    at = kernel(places, [owner, core], [pivots.reshape(-1, 128)], (2, 8, 128), dtype=jnp.int32)
    permuted = kernel(permute, [], [at, own, other], (columns, row_block))
    return kernel(finish, [], [pieces, permuted], (columns, row_block), vmem_out=False)


def solution(mesh):
    fine = Mesh(mesh.devices.reshape(tuple(AXES.values())), tuple(AXES))
    spec = P(BULK, OWNER)

    return jax.shard_map(shards, mesh=fine, in_specs=(spec, P(), spec, spec), out_specs=spec, check_vma=False)
```

```python
import jax
import jax.numpy as jnp
from jax import lax
from jax.experimental import pallas as pl
from jax.experimental.pallas import tpu as pltpu
from jax.sharding import Mesh, PartitionSpec as P


BULK = ("x", "y", "zh")
OWNER = ("z1", "z0", "c")
AXES = {"x": 8, "y": 8, "zh": 2, "z1": 2, "z0": 2, "c": 2}
SWAP = [(0, 1), (1, 0)]
VMEM = pl.BlockSpec(memory_space=pltpu.VMEM)
SMEM = pl.BlockSpec(memory_space=pltpu.SMEM)


def kernel(body, scalars, arrays, out, dtype=jnp.float32, vmem_out=True):
    arrays = [pltpu.with_memory_space_constraint(a, pltpu.VMEM) for a in arrays]
    return pl.pallas_call(
        body,
        out_shape=pltpu.VMEM(out, dtype) if vmem_out else jax.ShapeDtypeStruct(out, dtype),
        in_specs=[SMEM] * len(scalars) + [VMEM] * len(arrays),
        out_specs=VMEM,
    )(*scalars, *arrays)


def copies(zh_ref, own_ref, other_ref, out_ref):
    zh = zh_ref[0]
    for x in range(8):
        for z0 in range(2):
            rows = slice(z0 * 32, z0 * 32 + 32)
            out_ref[x, z0, zh] = own_ref[rows]
            out_ref[x, z0, 1 - zh] = other_ref[rows]


def repeat(block_ref, out_ref):
    for y in range(8):
        out_ref[y] = block_ref[...]


def line(z0_ref, z1_ref, own_ref, near_ref, far_ref, far_near_ref, out_ref):
    z0, z1 = z0_ref[0], z1_ref[0]
    out_ref[2 * z1 + z0] = own_ref[...]
    out_ref[2 * z1 + 1 - z0] = near_ref[...]
    out_ref[2 * (1 - z1) + z0] = far_ref[...]
    out_ref[2 * (1 - z1) + 1 - z0] = far_near_ref[...]


def product(parity_ref, z0_ref, upper_ref, swapped_ref, lower_ref, out_ref):
    parity, z0 = parity_ref[0], z0_ref[0]
    for z in range(4):
        halves = []
        for half in range(2):
            dots = [
                lax.dot_general(
                    ref[:, half * 16 : half * 16 + 16, :].reshape(128, 256),
                    lower_ref[2 * z + parity, index],
                    (((1,), (1,)), ((), ())),
                    preferred_element_type=jnp.float32,
                )
                for ref, index in ((upper_ref, z0), (swapped_ref, 1 - z0))
            ]
            halves.append(dots[0] + dots[1])
        out_ref[z] = jnp.concatenate(halves, axis=1).reshape(8, 16, 128)


def add(left_ref, right_ref, out_ref):
    out_ref[...] = left_ref[...] + right_ref[...]


def places(owner_ref, core_ref, pivots_ref, out_ref):
    index = pivots_ref[pl.ds(pl.multiple_of(owner_ref[0] * 8, 8), 8), :]
    side = ((index >> 10) & 1) ^ core_ref[0]
    out_ref[0] = index & 127
    out_ref[1] = side * 32 + (index >> 11) * 8 + ((index >> 7) & 7)


def permute(places_ref, own_ref, other_ref, out_ref):
    def block(b, _):
        lane = jnp.broadcast_to(places_ref[0, pl.ds(b, 1), :], (32, 128))
        key = jnp.broadcast_to(places_ref[1, pl.ds(b, 1), :], (32, 128))
        found = jnp.zeros((32, 128), jnp.float32)
        for k in range(64):
            ref = own_ref if k < 32 else other_ref
            source = ref[(k % 32) // 8, :, (k % 8) * 128 : (k % 8 + 1) * 128]
            found = jnp.where(key == k, jnp.take_along_axis(source, lane, axis=1, mode="promise_in_bounds"), found)
        out_ref[:, pl.ds(pl.multiple_of(b * 128, 128), 128)] = found
        return 0

    lax.fori_loop(0, 8, block, 0)


def finish(pieces_ref, permuted_ref, out_ref):
    quarter = lax.broadcasted_iota(jnp.int32, (16, 128), 1) // 32
    for y in range(8):
        at = slice(y * 128, (y + 1) * 128)
        sums = [pieces_ref[0, z0, y] + pieces_ref[1, z0, y] for z0 in range(2)]
        for half in range(2):
            rows = slice(half * 16, half * 16 + 16)
            update = sums[0]
            for q in range(4):
                zh, z0 = q // 2, q % 2
                shift = (q * 32 - half * 64 - zh * 32) % 128
                moved = pltpu.roll(sums[z0], shift, 1) if shift else sums[z0]
                update = jnp.where(quarter == q, moved, update)
            out_ref[rows, at] = permuted_ref[rows, at] - update


def shards(slab_cols, pivots, lower_panels, upper_rows):
    core, zh, owner = (lax.axis_index(axes).reshape(1) for axes in ("c", "zh", OWNER))
    z0, z1 = (lax.axis_index(axis).reshape(1) for axis in ("z0", "z1"))
    columns, row_block = slab_cols.shape
    inner = upper_rows.shape[1]

    upper = kernel(repeat, [], [upper_rows], (8, columns, inner), dtype=jnp.bfloat16)
    upper = lax.all_to_all(upper, "y", 0, 0, tiled=True)
    swapped = lax.ppermute(upper, "z0", SWAP)
    paired = lax.ppermute(lower_panels, "zh", SWAP)
    lower = kernel(copies, [zh], [lower_panels, paired], (8, 2, 2, 32, inner), dtype=jnp.bfloat16)
    lower = lax.all_to_all(lower.reshape(16, 64, inner), ("x", "z0"), 0, 0, tiled=True).reshape(8, 2, 64, inner)

    near = lax.ppermute(slab_cols, "z0", SWAP)
    far = lax.ppermute(slab_cols, "z1", SWAP)
    far_near = lax.ppermute(near, "z1", SWAP)
    own = kernel(line, [z0, z1], [slab_cols, near, far, far_near], (4, columns, row_block))
    other = lax.ppermute(own, "c", SWAP)

    def partial_value(parity):
        return kernel(product, [parity, z0], [upper, swapped, lower], (4, 8, 16, 128))

    received = lax.ppermute(partial_value(1 - core), "c", SWAP)
    kept = kernel(add, [], [received, partial_value(core)], (4, 8, 16, 128))

    pieces = lax.all_to_all(kept.reshape(32, 16, 128), ("z1", "z0", "y"), 0, 0, tiled=True)
    pieces = pieces.reshape(2, 2, 8, 16, 128)

    at = kernel(places, [owner, core], [pivots.reshape(-1, 128)], (2, 8, 128), dtype=jnp.int32)
    permuted = kernel(permute, [], [at, own, other], (columns, row_block))
    return kernel(finish, [], [pieces, permuted], (columns, row_block), vmem_out=False)


def solution(mesh):
    fine = Mesh(mesh.devices.reshape(tuple(AXES.values())), tuple(AXES))
    spec = P(BULK, OWNER)

    return jax.shard_map(shards, mesh=fine, in_specs=(spec, P(), spec, spec), out_specs=spec, check_vma=False)
```

```python
import jax
import jax.numpy as jnp
from jax import lax
from jax.experimental import pallas as pl
from jax.experimental.pallas import tpu as pltpu
from jax.sharding import Mesh, PartitionSpec as P


BULK = ("x", "y", "zh")
OWNER = ("z1", "z0", "c")
AXES = {"x": 8, "y": 8, "zh": 2, "z1": 2, "z0": 2, "c": 2}
SWAP = [(0, 1), (1, 0)]
VMEM = pl.BlockSpec(memory_space=pltpu.VMEM)
SMEM = pl.BlockSpec(memory_space=pltpu.SMEM)


def kernel(body, scalars, arrays, out, dtype=jnp.float32, vmem_in=True, vmem_out=True):
    if vmem_in:
        arrays = [pltpu.with_memory_space_constraint(a, pltpu.VMEM) for a in arrays]
    return pl.pallas_call(
        body,
        out_shape=pltpu.VMEM(out, dtype) if vmem_out else jax.ShapeDtypeStruct(out, dtype),
        in_specs=[SMEM] * len(scalars) + [VMEM] * len(arrays),
        out_specs=VMEM,
    )(*scalars, *arrays)


def copies(zh_ref, own_ref, other_ref, out_ref):
    zh = zh_ref[0]
    for x in range(8):
        for z0 in range(2):
            rows = slice(z0 * 32, z0 * 32 + 32)
            out_ref[x, z0, zh] = own_ref[rows]
            out_ref[x, z0, 1 - zh] = other_ref[rows]


def repeat(block_ref, out_ref):
    for y in range(8):
        out_ref[y] = block_ref[...]


def line(z0_ref, z1_ref, own_ref, near_ref, far_ref, far_near_ref, out_ref):
    z0, z1 = z0_ref[0], z1_ref[0]
    out_ref[2 * z1 + z0] = own_ref[...]
    out_ref[2 * z1 + 1 - z0] = near_ref[...]
    out_ref[2 * (1 - z1) + z0] = far_ref[...]
    out_ref[2 * (1 - z1) + 1 - z0] = far_near_ref[...]


def product(parity_ref, z0_ref, upper_ref, swapped_ref, lower_ref, out_ref):
    parity, z0 = parity_ref[0], z0_ref[0]
    for z in range(4):
        halves = []
        for half in range(2):
            dots = [
                lax.dot_general(
                    ref[:, half * 16 : half * 16 + 16, :].reshape(128, 256),
                    lower_ref[2 * z + parity, index],
                    (((1,), (1,)), ((), ())),
                    preferred_element_type=jnp.float32,
                )
                for ref, index in ((upper_ref, z0), (swapped_ref, 1 - z0))
            ]
            halves.append(dots[0] + dots[1])
        out_ref[z] = jnp.concatenate(halves, axis=1).reshape(8, 16, 128)


def add(left_ref, right_ref, out_ref):
    out_ref[...] = left_ref[...] + right_ref[...]


def places(owner_ref, core_ref, pivots_ref, out_ref):
    index = pivots_ref[pl.ds(pl.multiple_of(owner_ref[0] * 8, 8), 8), :]
    side = ((index >> 10) & 1) ^ core_ref[0]
    out_ref[0] = index & 127
    out_ref[1] = side * 32 + (index >> 11) * 8 + ((index >> 7) & 7)


def permute(places_ref, own_ref, other_ref, out_ref):
    def block(b, _):
        lane = jnp.broadcast_to(places_ref[0, pl.ds(b, 1), :], (32, 128))
        key = jnp.broadcast_to(places_ref[1, pl.ds(b, 1), :], (32, 128))
        found = jnp.zeros((32, 128), jnp.float32)
        for k in range(64):
            ref = own_ref if k < 32 else other_ref
            source = ref[(k % 32) // 8, :, (k % 8) * 128 : (k % 8 + 1) * 128]
            found = jnp.where(key == k, jnp.take_along_axis(source, lane, axis=1, mode="promise_in_bounds"), found)
        out_ref[:, pl.ds(pl.multiple_of(b * 128, 128), 128)] = found
        return 0

    lax.fori_loop(0, 8, block, 0)


def finish(pieces_ref, permuted_ref, out_ref):
    quarter = lax.broadcasted_iota(jnp.int32, (16, 128), 1) // 32
    for y in range(8):
        at = slice(y * 128, (y + 1) * 128)
        sums = [pieces_ref[0, z0, y] + pieces_ref[1, z0, y] for z0 in range(2)]
        for half in range(2):
            rows = slice(half * 16, half * 16 + 16)
            update = sums[0]
            for q in range(4):
                zh, z0 = q // 2, q % 2
                shift = (q * 32 - half * 64 - zh * 32) % 128
                moved = pltpu.roll(sums[z0], shift, 1) if shift else sums[z0]
                update = jnp.where(quarter == q, moved, update)
            out_ref[rows, at] = permuted_ref[rows, at] - update


def shards(slab_cols, pivots, lower_panels, upper_rows):
    core, zh, owner = (lax.axis_index(axes).reshape(1) for axes in ("c", "zh", OWNER))
    z0, z1 = (lax.axis_index(axis).reshape(1) for axis in ("z0", "z1"))
    columns, row_block = slab_cols.shape
    inner = upper_rows.shape[1]

    upper = kernel(repeat, [], [upper_rows], (8, columns, inner), dtype=jnp.bfloat16, vmem_in=False)
    upper = lax.all_to_all(upper, "y", 0, 0, tiled=True)
    swapped = lax.ppermute(upper, "z0", SWAP)
    paired = lax.ppermute(lower_panels, "zh", SWAP)
    lower = kernel(copies, [zh], [lower_panels, paired], (8, 2, 2, 32, inner), dtype=jnp.bfloat16)
    lower = lax.all_to_all(lower.reshape(16, 64, inner), ("x", "z0"), 0, 0, tiled=True).reshape(8, 2, 64, inner)

    near = lax.ppermute(slab_cols, "z0", SWAP)
    far = lax.ppermute(slab_cols, "z1", SWAP)
    far_near = lax.ppermute(near, "z1", SWAP)
    own = kernel(line, [z0, z1], [slab_cols, near, far, far_near], (4, columns, row_block))
    other = lax.ppermute(own, "c", SWAP)

    def partial_value(parity):
        return kernel(product, [parity, z0], [upper, swapped, lower], (4, 8, 16, 128))

    received = lax.ppermute(partial_value(1 - core), "c", SWAP)
    kept = kernel(add, [], [received, partial_value(core)], (4, 8, 16, 128))

    pieces = lax.all_to_all(kept.reshape(32, 16, 128), ("z1", "z0", "y"), 0, 0, tiled=True)
    pieces = pieces.reshape(2, 2, 8, 16, 128)

    at = kernel(places, [owner, core], [pivots.reshape(-1, 128)], (2, 8, 128), dtype=jnp.int32)
    permuted = kernel(permute, [], [at, own, other], (columns, row_block))
    return kernel(finish, [], [pieces, permuted], (columns, row_block), vmem_out=False)


def solution(mesh):
    fine = Mesh(mesh.devices.reshape(tuple(AXES.values())), tuple(AXES))
    spec = P(BULK, OWNER)

    return jax.shard_map(shards, mesh=fine, in_specs=(spec, P(), spec, spec), out_specs=spec, check_vma=False)
```

```python
import jax
import jax.numpy as jnp
from jax import lax
from jax.experimental import pallas as pl
from jax.experimental.pallas import tpu as pltpu
from jax.sharding import Mesh, PartitionSpec as P


BULK = ("x", "y", "zh")
OWNER = ("z1", "z0", "c")
AXES = {"x": 8, "y": 8, "zh": 2, "z1": 2, "z0": 2, "c": 2}
SWAP = [(0, 1), (1, 0)]
VMEM = pl.BlockSpec(memory_space=pltpu.VMEM)
SMEM = pl.BlockSpec(memory_space=pltpu.SMEM)


def kernel(body, scalars, arrays, out, dtype=jnp.float32, vmem_in=True, vmem_out=True):
    if vmem_in:
        arrays = [pltpu.with_memory_space_constraint(a, pltpu.VMEM) for a in arrays]
    return pl.pallas_call(
        body,
        out_shape=pltpu.VMEM(out, dtype) if vmem_out else jax.ShapeDtypeStruct(out, dtype),
        in_specs=[SMEM] * len(scalars) + [VMEM] * len(arrays),
        out_specs=VMEM,
    )(*scalars, *arrays)


def halves(zh_ref, z0_ref, own_ref, other_ref, out_ref):
    zh, rows = zh_ref[0], pl.ds(pl.multiple_of((1 - z0_ref[0]) * 32, 32), 32)
    out_ref[zh] = own_ref[rows, :]
    out_ref[1 - zh] = other_ref[rows, :]


def copies(zh_ref, z0_ref, own_ref, other_ref, got_ref, out_ref):
    zh, z0 = zh_ref[0], z0_ref[0]
    rows = pl.ds(pl.multiple_of(z0 * 32, 32), 32)
    for x in range(8):
        out_ref[x, z0, zh] = own_ref[rows, :]
        out_ref[x, z0, 1 - zh] = other_ref[rows, :]
        out_ref[x, 1 - z0] = got_ref[...]


def repeat(block_ref, out_ref):
    for y in range(8):
        out_ref[y] = block_ref[...]


def line(z0_ref, z1_ref, own_ref, near_ref, far_ref, far_near_ref, out_ref):
    z0, z1 = z0_ref[0], z1_ref[0]
    out_ref[2 * z1 + z0] = own_ref[...]
    out_ref[2 * z1 + 1 - z0] = near_ref[...]
    out_ref[2 * (1 - z1) + z0] = far_ref[...]
    out_ref[2 * (1 - z1) + 1 - z0] = far_near_ref[...]


def product(parity_ref, z0_ref, upper_ref, swapped_ref, lower_ref, out_ref):
    parity, z0 = parity_ref[0], z0_ref[0]
    for z in range(4):
        halves = []
        for half in range(2):
            dots = [
                lax.dot_general(
                    ref[:, half * 16 : half * 16 + 16, :].reshape(128, 256),
                    lower_ref[2 * z + parity, index],
                    (((1,), (1,)), ((), ())),
                    preferred_element_type=jnp.float32,
                )
                for ref, index in ((upper_ref, z0), (swapped_ref, 1 - z0))
            ]
            halves.append(dots[0] + dots[1])
        out_ref[z] = jnp.concatenate(halves, axis=1).reshape(8, 16, 128)


def add(left_ref, right_ref, out_ref):
    out_ref[...] = left_ref[...] + right_ref[...]


def places(owner_ref, core_ref, pivots_ref, out_ref):
    index = pivots_ref[pl.ds(pl.multiple_of(owner_ref[0] * 8, 8), 8), :]
    side = ((index >> 10) & 1) ^ core_ref[0]
    out_ref[0] = index & 127
    out_ref[1] = side * 32 + (index >> 11) * 8 + ((index >> 7) & 7)


def permute(places_ref, own_ref, other_ref, out_ref):
    def block(b, _):
        lane = jnp.broadcast_to(places_ref[0, pl.ds(b, 1), :], (32, 128))
        key = jnp.broadcast_to(places_ref[1, pl.ds(b, 1), :], (32, 128))
        found = jnp.zeros((32, 128), jnp.float32)
        for k in range(64):
            ref = own_ref if k < 32 else other_ref
            source = ref[(k % 32) // 8, :, (k % 8) * 128 : (k % 8 + 1) * 128]
            found = jnp.where(key == k, jnp.take_along_axis(source, lane, axis=1, mode="promise_in_bounds"), found)
        out_ref[:, pl.ds(pl.multiple_of(b * 128, 128), 128)] = found
        return 0

    lax.fori_loop(0, 8, block, 0)


def finish(pieces_ref, permuted_ref, out_ref):
    quarter = lax.broadcasted_iota(jnp.int32, (16, 128), 1) // 32
    for y in range(8):
        at = slice(y * 128, (y + 1) * 128)
        sums = [pieces_ref[0, z0, y] + pieces_ref[1, z0, y] for z0 in range(2)]
        for half in range(2):
            rows = slice(half * 16, half * 16 + 16)
            update = sums[0]
            for q in range(4):
                zh, z0 = q // 2, q % 2
                shift = (q * 32 - half * 64 - zh * 32) % 128
                moved = pltpu.roll(sums[z0], shift, 1) if shift else sums[z0]
                update = jnp.where(quarter == q, moved, update)
            out_ref[rows, at] = permuted_ref[rows, at] - update


def shards(slab_cols, pivots, lower_panels, upper_rows):
    core, zh, owner = (lax.axis_index(axes).reshape(1) for axes in ("c", "zh", OWNER))
    z0, z1 = (lax.axis_index(axis).reshape(1) for axis in ("z0", "z1"))
    columns, row_block = slab_cols.shape
    inner = upper_rows.shape[1]

    upper = kernel(repeat, [], [upper_rows], (8, columns, inner), dtype=jnp.bfloat16, vmem_in=False)
    upper = lax.all_to_all(upper, "y", 0, 0, tiled=True)
    swapped = lax.ppermute(upper, "z0", SWAP)
    paired = lax.ppermute(lower_panels, "zh", SWAP)
    given = kernel(halves, [zh, z0], [lower_panels, paired], (2, 32, inner), dtype=jnp.bfloat16)
    got = lax.ppermute(given, "z0", SWAP)
    lower = kernel(copies, [zh, z0], [lower_panels, paired, got], (8, 2, 2, 32, inner), dtype=jnp.bfloat16)
    lower = lax.all_to_all(lower.reshape(8, 128, inner), "x", 0, 0, tiled=True).reshape(8, 2, 64, inner)

    near = lax.ppermute(slab_cols, "z0", SWAP)
    far = lax.ppermute(slab_cols, "z1", SWAP)
    far_near = lax.ppermute(near, "z1", SWAP)
    own = kernel(line, [z0, z1], [slab_cols, near, far, far_near], (4, columns, row_block))
    other = lax.ppermute(own, "c", SWAP)

    def partial_value(parity):
        return kernel(product, [parity, z0], [upper, swapped, lower], (4, 8, 16, 128))

    received = lax.ppermute(partial_value(1 - core), "c", SWAP)
    kept = kernel(add, [], [received, partial_value(core)], (4, 8, 16, 128))

    pieces = lax.all_to_all(kept.reshape(32, 16, 128), ("z1", "z0", "y"), 0, 0, tiled=True)
    pieces = pieces.reshape(2, 2, 8, 16, 128)

    at = kernel(places, [owner, core], [pivots.reshape(-1, 128)], (2, 8, 128), dtype=jnp.int32)
    permuted = kernel(permute, [], [at, own, other], (columns, row_block))
    return kernel(finish, [], [pieces, permuted], (columns, row_block), vmem_out=False)


def solution(mesh):
    fine = Mesh(mesh.devices.reshape(tuple(AXES.values())), tuple(AXES))
    spec = P(BULK, OWNER)

    return jax.shard_map(shards, mesh=fine, in_specs=(spec, P(), spec, spec), out_specs=spec, check_vma=False)
```
